32 devices in a mesh: rows: 4 (over y, x), cols: 8 (over z, core).
Axes of the slice: x: 2, y: 2, z: 4, core: 2. Of those that a mesh axis runs over, the one named last changes fastest.
Arguments:
- values: bfloat16 [2, 2048, 65536], P(None, 'rows', 'cols'), may hold values from -0.0234375 to 0.0234375
- block_ids: int32 [2, 4, 8, 64], P(None, 'rows', 'cols'), may hold values from -1 to 255, as said below
- labels: int32 [2, 2048], P(None, 'rows'), may hold values from 0 to 1
- table: float32 [256, 128, 128], P('cols'), may hold values from -3 to 3
- table_acc: float32 [256, 128, 128], P('cols'), may hold values from 1e-05 to 0.001
- lin: float32 [256, 128], P('cols'), may hold values from -3 to 3
- lin_acc: float32 [256, 128], P('cols'), may hold values from 1e-05 to 0.001
Outputs:
- new_table: float32 [256, 128, 128], P('cols')
- new_lin: float32 [256, 128], P('cols')
- logits: float32 [2, 2048], P(None, 'rows')
The draws below stay inside these ranges and needn't reach their ends.
Inputs may be any that keep to these rules, and one draw needn't show every extreme that they name: `block_ids`: each list holds its active ids first and -1 after them; active ids of one list are distinct; at most 16 active ids of one list lie in one owner range (id // 32); a list has 48 to 64 active ids and some list has 64; in each minibatch one owner range, drawn from the seed, gets exactly 16 ids from every list.
All inputs are finite; a program needn't handle non-finite values.
Results may differ from the reference program's by a relative error of at most 0.0049.
Values may be sent and summed in bfloat16 or wider, within the bound.
No kernel may reach another device: no remote copies, remote signals or barrier semaphores. Data moves between devices by JAX's collectives and lax.ppermute only.
A program may use at most 128 MiB of HBM per device.

```python
import math
import jax
import jax.numpy as jnp
from jax import lax

K = 128
BW = 128
MAXB = 64
ITERS = 2
EX = 512
BLK_DEV = 32
CAP = 16
NBLK = 256
EXAMPLES = 2048
N_ROWS = 4
N_COLS = 8


def one_list(list_key, hot_owner, filled):
    count_key, order_key, base_key, mix_key = jax.random.split(list_key, 4)
    slot_count = N_COLS * CAP
    count = jnp.where(filled, MAXB, jax.random.randint(count_key, (), 3 * MAXB // 4, MAXB + 1))
    order = jax.random.permutation(order_key, slot_count)
    is_hot = order // CAP == hot_owner
    ranking = jnp.where(is_hot, 0, slot_count) + jnp.arange(slot_count)
    chosen = order[jnp.argsort(ranking)][:MAXB]
    owner_of = chosen // CAP
    rank_in = chosen % CAP
    offsets = jax.random.randint(base_key, (N_COLS,), 0, BLK_DEV)
    local = (offsets[owner_of] + rank_in * (BLK_DEV // CAP)) % BLK_DEV
    blocks = owner_of * BLK_DEV + local
    position = jnp.arange(MAXB)
    shuffle = jax.random.permutation(mix_key, MAXB)
    placing = jnp.where(position < count, shuffle, MAXB + position)
    arranged = blocks[jnp.argsort(placing)]
    return jnp.where(position < count, arranged, -1).astype(jnp.int32)


def draw_block_ids(key, part):
    list_total = ITERS * N_ROWS * N_COLS
    hot_key, list_key = jax.random.split(jax.random.fold_in(key, 7))
    hot = jax.random.randint(hot_key, (ITERS,), 0, N_COLS)
    hot_each = jnp.repeat(hot, N_ROWS * N_COLS)
    list_keys = jax.random.split(list_key, list_total)
    filled = jnp.arange(list_total) % (N_ROWS * N_COLS) == 0
    lists = jax.vmap(one_list)(list_keys, hot_each, filled)
    return lists.reshape(ITERS, N_ROWS, N_COLS, MAXB)


def place_ends(drawn, key, smallest, high):
    dims = drawn.shape
    index_at = [jax.random.randint(jax.random.fold_in(key, axis), (), 0, dims[axis]) for axis in range(len(dims))]
    drawn = drawn.at[tuple(index_at)].set(smallest)
    longest = dims.index(max(dims))
    index_at[longest] = (index_at[longest] + 1) % dims[longest]
    return drawn.at[tuple(index_at)].set(high)


def level_of(key, shape, cuts, low, largest):
    loudness = 1.0
    for dim, blocks in cuts:
        heights = jax.random.uniform(jax.random.fold_in(jax.random.fold_in(key, 6), dim), (blocks,), jnp.float32, low / len(cuts), largest / len(cuts))
        loudness = loudness * jnp.repeat(jnp.exp(heights), shape[dim] // blocks).reshape((-1,) + (1,) * (len(shape) - 1 - dim))
    return loudness


def scatter_about(own_key, shape, scale, limit, shards=(), kind=jnp.bfloat16):
    level = level_of(own_key, shape, shards, -0.22, 0.18) if shards else 1.0
    drawn = jax.random.normal(own_key, shape, jnp.float32) * scale * level
    return jnp.minimum(jnp.maximum(drawn, -limit), limit).astype(kind)


def setup_inputs(seed: int = 0) -> dict:
    keys = jax.random.split(jax.random.key(seed), 8)
    return {
        "values": scatter_about(keys[0], (ITERS, EXAMPLES, N_COLS * MAXB * BW), (N_COLS * MAXB * BW) ** -0.5, 0.0234375, ((1, 4), (2, 8))),
        "block_ids": draw_block_ids(jax.random.fold_in(keys[7], 71), 0),
        "labels": place_ends(jax.random.randint(keys[2], (ITERS, EXAMPLES), 0, 2), jax.random.fold_in(keys[2], 1), 0, 1).astype(jnp.int32),
        "table": scatter_about(keys[3], (NBLK, BW, K), 0.5, 3.0, ((0, 8),), jnp.float32),
        "table_acc": jnp.clip(jnp.exp(math.log(0.001) - 4.6051703 * jax.random.uniform(keys[4], (NBLK, BW, K), jnp.float32) ** level_of(keys[4], (NBLK, BW, K), ((0, 8),), -0.2, 0.2)), 9.999999747378752e-06, 0.001),
        "lin": scatter_about(keys[5], (NBLK, BW), 0.5, 3.0, ((0, 8),), jnp.float32),
        "lin_acc": jnp.clip(jnp.exp(math.log(0.001) - 4.6051703 * jax.random.uniform(keys[6], (NBLK, BW), jnp.float32) ** level_of(keys[6], (NBLK, BW), ((0, 8),), -0.2, 0.2)), 9.999999747378752e-06, 0.001),
    }


learn_rate = 0.2

def masked_rows(features, present):
    mask = jnp.repeat(present, BW)
    return jnp.where(mask[None, :], features, jnp.zeros((), jnp.bfloat16))

def pulled(block_list, table, lin):
    present = block_list >= 0
    safe = jnp.where(present, block_list, 0)
    factor_rows = table[safe].astype(jnp.bfloat16).reshape(MAXB * BW, K)
    linear_rows = lin[safe].astype(jnp.bfloat16).reshape(MAXB * BW)
    return (present, factor_rows, linear_rows)

def partials(features, block_list, table, lin):
    present, factor_rows, linear_rows = pulled(block_list, table, lin)
    active = masked_rows(features, present)
    xv_part = jnp.dot(active, factor_rows, preferred_element_type=jnp.float32)
    factor_float = factor_rows.astype(jnp.float32)
    sumsq = lax.optimization_barrier(jnp.sum(factor_float * factor_float, axis=1))
    active_float = active.astype(jnp.float32)
    sq_part = lax.optimization_barrier(jnp.sum(active_float * active_float * sumsq[None, :], axis=1))
    lin_part = jnp.dot(active, linear_rows, preferred_element_type=jnp.float32)
    return (xv_part, sq_part, lin_part)

def gradients(features, block_list, table, lin, slope, weighted):
    present, factor_rows, linear_rows = pulled(block_list, table, lin)
    active = masked_rows(features, present)
    grad_factor = lax.dot_general(active, weighted, (((0,), (0,)), ((), ())), preferred_element_type=jnp.float32)
    active_float = active.astype(jnp.float32)
    weight_sq = lax.optimization_barrier(jnp.sum(active_float * active_float * slope[:, None], axis=0))
    grad_factor = grad_factor - factor_rows.astype(jnp.float32) * weight_sq[:, None]
    grad_linear = lax.optimization_barrier(jnp.sum(active_float * slope[:, None], axis=0))
    return (grad_factor.astype(jnp.bfloat16).reshape(MAXB, BW, K), grad_linear.astype(jnp.bfloat16).reshape(MAXB, BW))

def reference(values, block_ids, labels, table, table_acc, lin, lin_acc):
    total_blocks = table.shape[0]
    logit_list = []
    for step in range(ITERS):
        grouped = values[step].reshape(N_ROWS, EX, N_COLS, MAXB * BW)
        grad_table = jnp.zeros(table.shape, jnp.float32)
        grad_lin = jnp.zeros(lin.shape, jnp.float32)
        row_logits = []
        for group in range(N_ROWS):
            group_values = grouped[group]
            group_ids = block_ids[step, group]

            def column_stats(column):
                features = lax.dynamic_index_in_dim(group_values, column, 1, False)
                block_list = lax.dynamic_index_in_dim(group_ids, column, 0, False)
                return partials(features, block_list, table, lin)
            xv_all, sq_all, lin_all = lax.map(column_stats, jnp.arange(N_COLS))
            xv_sum = lax.optimization_barrier(jnp.sum(xv_all, axis=0))
            logit = lax.optimization_barrier(jnp.sum(lin_all, axis=0)) + 0.5 * (lax.optimization_barrier(jnp.sum(xv_sum * xv_sum, axis=1)) - lax.optimization_barrier(jnp.sum(sq_all, axis=0)))
            label_rows = labels[step, group * EX:(group + 1) * EX].astype(jnp.float32)
            slope = jax.nn.sigmoid(logit) - label_rows
            weighted = (slope[:, None] * xv_sum).astype(jnp.bfloat16)

            def add_column(column, carry):
                gtab, glin = carry
                features = lax.dynamic_index_in_dim(group_values, column, 1, False)
                block_list = lax.dynamic_index_in_dim(group_ids, column, 0, False)
                tile_grad, lin_grad = gradients(features, block_list, table, lin, slope, weighted)
                target = jnp.where(block_list >= 0, block_list, total_blocks)
                gtab = gtab.at[target].add(tile_grad.astype(jnp.float32), mode='drop')
                glin = glin.at[target].add(lin_grad.astype(jnp.float32), mode='drop')
                return (gtab, glin)
            grad_table, grad_lin = lax.fori_loop(0, N_COLS, add_column, (grad_table, grad_lin))
            row_logits.append(logit)
        table_acc = table_acc + grad_table * grad_table
        table = table - learn_rate * grad_table / jnp.sqrt(table_acc)
        lin_acc = lin_acc + grad_lin * grad_lin
        lin = lin - learn_rate * grad_lin / jnp.sqrt(lin_acc)
        logit_list.append(jnp.concatenate(row_logits))
    return (table, lin, jnp.stack(logit_list))
```

```python
import functools

import jax
import jax.numpy as jnp
from jax import lax
from jax.experimental import pallas as pl
from jax.experimental.pallas import tpu as pltpu
from jax.sharding import PartitionSpec as P

learn_rate = 0.2
F32 = jnp.float32
BF16 = jnp.bfloat16
CHUNK = 8


VMEM = pl.BlockSpec(memory_space=pltpu.VMEM)
SMEM = pl.BlockSpec(memory_space=pltpu.SMEM)
ANY = pl.BlockSpec(memory_space=pl.ANY)


def locate(block, meta, blocks_dev, ring, sign):
    owner = block // blocks_dev
    home, core = owner // 2, owner % 2
    apart = lax.rem(sign * (home - meta[1]) + ring, ring)
    far = jnp.where(core == meta[2], 0, 1)
    return far * ring + apart, block % blocks_dev


def select_kernel(step, rows, ring, blocks_dev, listed, *refs):
    meta = refs[0]
    ids = refs[1 : 1 + rows]
    held = refs[1 + rows : 1 + rows + 2 * ring]
    outs = refs[1 + rows + 2 * ring : 1 + 2 * rows + 2 * ring]
    lin_out, pool, lin_pool, sems = refs[1 + 2 * rows + 2 * ring :]
    copies = [
        pltpu.make_async_copy(src, pool.at[i], sems.at[i]) for i, src in enumerate(held)
    ]
    for copy in copies:
        copy.start()
    for copy in copies:
        copy.wait()
    for i in range(2 * ring):
        lin_pool[i * blocks_dev : (i + 1) * blocks_dev] = pool[i, blocks_dev].astype(F32)
    for m in range(rows):

        def body(k, carry, m=m):
            block = ids[m][step, k]
            live = block >= 0
            at, inner = locate(jnp.where(live, block, 0), meta, blocks_dev, ring, -1)
            piece = pool[at, inner]
            outs[m][k] = jnp.where(live, piece, jnp.zeros_like(piece))
            if m == 0:
                row = lin_pool[pl.ds(at * blocks_dev + inner, 1), :]
                lin_out[pl.ds(k, 1), :] = jnp.where(live, row, 0.0)
            return carry

        lax.fori_loop(0, listed, body, 0, unroll=4)


def gather_tiles(meta, pieces, tiles, piece_rows, width):
    rows = len(pieces)
    for m in range(rows):
        start = jnp.bitwise_xor(meta[0], m) * piece_rows
        for i in range(CHUNK):
            at = pl.multiple_of(i * width + start, piece_rows)
            tiles[pl.ds(at, piece_rows), :] = pieces[m][i]


def forward_kernel(rows, ex, width, *refs):
    meta, values = refs[0], refs[1]
    pieces = refs[2 : 2 + rows]
    lin, keep, send, tiles, xv, extra, sq = refs[2 + rows :]
    here = pl.program_id(0)
    piece_rows = width // rows
    gather_tiles(meta, pieces, tiles, piece_rows, width)

    @pl.when(here == 0)
    def _():
        xv[...] = jnp.zeros_like(xv)
        extra[...] = jnp.zeros_like(extra)

    for i in range(CHUNK):
        tile = tiles[i * width : (i + 1) * width].astype(F32)
        flipped = (tile * tile).T
        sq[i : i + 1, :] = -0.5 * jnp.sum(flipped, axis=0, keepdims=True)
    xv[...] += jnp.dot(values[0], tiles[...], preferred_element_type=F32)
    group = 64

    def body(g, carry):
        at = pl.multiple_of(g * group, group)
        total = extra[pl.ds(at, group), :]
        for i in range(CHUNK):
            v = values[0, pl.ds(at, group), i * width : (i + 1) * width].astype(F32)
            total = total + v * (lin[i : i + 1, :] + v * sq[i : i + 1, :])
        extra[pl.ds(at, group), :] = total
        return carry

    lax.fori_loop(0, ex // group, body, 0)

    @pl.when(here == pl.num_programs(0) - 1)
    def _():
        half = ex // 2
        lanes = keep.shape[1]
        for out, mine in ((keep, meta[2]), (send, 1 - meta[2])):
            at = pl.multiple_of(mine * half, half)
            out[:half] = xv[pl.ds(at, half), :]
            tail = []
            for i in range(half // lanes):
                part = extra[pl.ds(pl.multiple_of(at + i * lanes, lanes), lanes), :]
                tail.append(jnp.sum(part.T, axis=0, keepdims=True))
            fill = out.shape[0] - half - len(tail)
            out[half:] = jnp.concatenate(tail + [jnp.zeros((fill, lanes), F32)], axis=0)


def backward_kernel(step, rows, ex, width, listed, *refs):
    meta, values = refs[0], refs[1]
    pieces = refs[2 : 2 + rows]
    mine, other, labels = refs[2 + rows : 5 + rows]
    logits = refs[5 + rows]
    outs = refs[6 + rows : 6 + 2 * rows]
    tiles, xvt, lhs, slope_col, lin_rows, grads = refs[6 + 2 * rows :]
    here = pl.program_id(0)
    piece_rows = width // rows
    half = ex // 2
    factors = mine.shape[1]
    gather_tiles(meta, pieces, tiles, piece_rows, width)

    @pl.when(here == 0)
    def _():
        for src, part in ((mine, meta[2]), (other, 1 - meta[2])):
            for i in range(half // factors):
                at = pl.multiple_of(part * half + i * factors, factors)
                flipped = src[i * factors : (i + 1) * factors, :].T
                logit = src[half + i : half + i + 1, :] + 0.5 * jnp.sum(
                    flipped * flipped, axis=0, keepdims=True
                )
                label = labels[step : step + 1, pl.ds(at, factors)].astype(F32)
                slope = jax.nn.sigmoid(logit) - label
                logits[:, pl.ds(at, factors)] = logit
                lhs[0:factors, pl.ds(at, factors)] = (slope * flipped).astype(BF16)
                high = slope.astype(BF16)
                left = slope - high.astype(F32)
                middle = left.astype(BF16)
                low = (left - middle.astype(F32)).astype(BF16)
                fill = jnp.zeros((lhs.shape[0] - factors - 3, factors), F32)
                lhs[factors:, pl.ds(at, factors)] = jnp.concatenate(
                    [high.astype(F32), middle.astype(F32), low.astype(F32), fill], axis=0
                ).astype(BF16)
                slope_col[pl.ds(at, factors), :] = jnp.broadcast_to(
                    slope, (factors, factors)
                ).T

    xvt[...] = jnp.dot(lhs[...], values[0], preferred_element_type=F32)
    group = 64

    def body(g, totals):
        at = pl.multiple_of(g * group, group)
        slope = slope_col[pl.ds(at, group), :]
        result = []
        for i in range(CHUNK):
            v = values[0, pl.ds(at, group), i * width : (i + 1) * width].astype(F32)
            term = (v * v * slope).reshape(group // 8, 8, width)
            result.append(totals[i] + jnp.sum(term, axis=0))
        return tuple(result)

    totals = lax.fori_loop(
        0, ex // group, body, tuple(jnp.zeros((8, width), F32) for _ in range(CHUNK))
    )
    row_list = []
    for i in range(CHUNK):
        cut = slice(i * width, (i + 1) * width)
        weight_sq = jnp.broadcast_to(
            jnp.sum(totals[i], axis=0, keepdims=True), (factors, width)
        ).T
        tile = tiles[cut].astype(F32)
        grads[...] = xvt[0:factors, cut].T - tile * weight_sq
        for m in range(rows):
            at = pl.multiple_of(jnp.bitwise_xor(meta[0], m) * piece_rows, piece_rows)
            outs[m][here * CHUNK + i] = grads[pl.ds(at, piece_rows), :].astype(BF16)
        row_list.append(
            xvt[factors : factors + 1, cut]
            + xvt[factors + 1 : factors + 2, cut]
            + xvt[factors + 2 : factors + 3, cut]
        )
    at = pl.multiple_of(here * CHUNK, CHUNK)
    lin_rows[pl.ds(at, CHUNK), :] = jnp.concatenate(row_list, axis=0)

    @pl.when(here == pl.num_programs(0) - 1)
    def _():
        for m in range(rows):
            for i in range(listed // piece_rows):
                outs[m][listed + i] = lin_rows[
                    i * piece_rows : (i + 1) * piece_rows
                ].astype(BF16)


def collect_kernel(step, rows, ring, blocks_dev, listed, *refs):
    meta = refs[0]
    ids = refs[1 : 1 + rows]
    pieces = refs[1 + rows : 1 + 2 * rows]
    keep, send, dense, dense_lin, lin_rows = refs[1 + 2 * rows :]
    piece_rows = dense.shape[2]
    dense[...] = jnp.zeros_like(dense)
    dense_lin[...] = jnp.zeros_like(dense_lin)
    for m in range(rows):
        order = m
        for i in range(listed // piece_rows):
            lin_rows[order * listed + i * piece_rows : order * listed + (i + 1) * piece_rows] = (
                pieces[m][listed + i].astype(F32)
            )

    def add(source, block, k):
        @pl.when(block >= 0)
        def _():
            at, inner = locate(block, meta, blocks_dev, ring, 1)
            dense[at, inner] += source[k].astype(F32)

    def add_lin(m, block, k):
        @pl.when(block >= 0)
        def _():
            at, inner = locate(block, meta, blocks_dev, ring, 1)
            row = pl.ds(at * blocks_dev + inner, 1)
            dense_lin[row, :] += lin_rows[pl.ds(m * listed + k, 1), :]

    for m in range(rows):

        def body(k, carry, m=m):
            add(pieces[m], ids[m][step, k], k)
            return carry

        lax.fori_loop(0, listed, body, 0, unroll=4)
    for group in range(rows):
        for m in range(rows):

            @pl.when(jnp.bitwise_xor(meta[0], m) == group)
            def _(m=m):
                def body(k, carry):
                    add_lin(m, ids[m][step, k], k)
                    return carry

                lax.fori_loop(0, listed, body, 0, unroll=4)

    for s in range(ring):
        near = slice(s * blocks_dev, (s + 1) * blocks_dev)
        far = slice((ring + s) * blocks_dev, (ring + s + 1) * blocks_dev)
        keep[s, 0:blocks_dev] = dense[s]
        keep[s, blocks_dev] = dense_lin[near]
        send[s, 0:blocks_dev] = dense[ring + s].astype(BF16)
        send[s, blocks_dev] = dense_lin[far].astype(BF16)


def finish_kernel(rows, *refs):
    meta, table = refs[0], refs[1]
    deltas = refs[2 : 2 + rows]
    out = refs[2 + rows]
    piece_rows = deltas[0].shape[1]
    for m in range(rows):
        at = pl.multiple_of(jnp.bitwise_xor(meta[0], m) * piece_rows, piece_rows)
        out[:, pl.ds(at, piece_rows), :] = table[:, pl.ds(at, piece_rows), :] - deltas[m][
            ...
        ].astype(F32)


def local(rows, cols, values, block_ids, labels, table, table_acc, lin, lin_acc):
    steps, ex, depth = values.shape
    listed = block_ids.shape[3]
    blocks_dev, width, factors = table.shape
    ring = cols // 2
    piece_rows = width // rows
    assert factors == width and blocks_dev == piece_rows and listed % CHUNK == 0

    row = lax.axis_index("rows")
    col = lax.axis_index("cols")
    meta = jnp.stack([row, col // 2, col % 2]).astype(jnp.int32)

    swap = [(c, c ^ 1) for c in range(cols)]

    def across(x, m):
        return lax.ppermute(x, "rows", [(r, r ^ m) for r in range(rows)])

    def around(x, s):
        return lax.ppermute(
            x, "cols", [(c, (c // 2 + s) % ring * 2 + c % 2) for c in range(cols)]
        )

    def beside(x, bit):
        return lax.ppermute(x, "cols", [(c, (c // 2 ^ bit) * 2 + c % 2) for c in range(cols)])

    def core(x):
        return lax.ppermute(x, "cols", swap)

    my_ids = block_ids.reshape(steps, listed)
    ids = [my_ids] + [across(my_ids, m) for m in range(1, rows)]
    base = lax.dynamic_slice_in_dim(table, row * piece_rows, piece_rows, 1)
    quarter = base
    quarter_acc = lax.dynamic_slice_in_dim(table_acc, row * piece_rows, piece_rows, 1)
    half_rows = ex // 2 + -(-(ex // 2 // factors) // 8) * 8
    piece = jax.ShapeDtypeStruct((listed, piece_rows, factors), BF16)
    tail = listed // piece_rows
    pushed = jax.ShapeDtypeStruct((listed + tail, piece_rows, factors), BF16)
    half = jax.ShapeDtypeStruct((half_rows, factors), F32)
    chunk_spec = pl.BlockSpec((CHUNK, piece_rows, factors), lambda i: (i, 0, 0))
    grid = listed // CHUNK
    logit_list = []

    for step in range(steps):
        values_spec = pl.BlockSpec((1, ex, CHUNK * width), lambda i, step=step: (step, 0, i))
        parcel = jnp.concatenate([quarter.astype(BF16), lin.astype(BF16)[None]], axis=0)
        near = [parcel] + [around(parcel, s) for s in range(1, ring)]
        far = [core(x) for x in near]
        *picked, lin_rows = pl.pallas_call(
            functools.partial(select_kernel, step, rows, ring, blocks_dev, listed),
            out_shape=[piece] * rows + [jax.ShapeDtypeStruct((listed, factors), F32)],
            in_specs=[SMEM] * (1 + rows) + [ANY] * (2 * ring),
            out_specs=[VMEM] * (rows + 1),
            scratch_shapes=[
                pltpu.VMEM((2 * ring, blocks_dev + 1, piece_rows, factors), BF16),
                pltpu.VMEM((2 * ring * blocks_dev, factors), F32),
                pltpu.SemaphoreType.DMA((2 * ring,)),
            ],
            name="select",
        )(meta, *ids, *near, *far)
        pieces = [picked[0]] + [across(picked[m], m) for m in range(1, rows)]
        keep, send = pl.pallas_call(
            functools.partial(forward_kernel, rows, ex, width),
            out_shape=[half, half],
            grid=(grid,),
            in_specs=[SMEM, values_spec]
            + [chunk_spec] * rows
            + [pl.BlockSpec((CHUNK, factors), lambda i: (i, 0))],
            out_specs=[pl.BlockSpec((half_rows, factors), lambda i: (0, 0))] * 2,
            scratch_shapes=[
                pltpu.VMEM((CHUNK * width, factors), BF16),
                pltpu.VMEM((ex, factors), F32),
                pltpu.VMEM((ex, factors), F32),
                pltpu.VMEM((CHUNK, width), F32),
            ],
            name="forward",
        )(meta, values, *pieces, lin_rows)
        mine = keep + core(send)
        bit = 1
        while bit < ring:
            mine = mine + beside(mine, bit)
            bit *= 2
        other = core(mine)
        logit, *outgoing = pl.pallas_call(
            functools.partial(backward_kernel, step, rows, ex, width, listed),
            out_shape=[jax.ShapeDtypeStruct((1, ex), F32)] + [pushed] * rows,
            grid=(grid,),
            in_specs=[SMEM, values_spec]
            + [chunk_spec] * rows
            + [pl.BlockSpec((half_rows, factors), lambda i: (0, 0))] * 2
            + [pl.BlockSpec((steps, ex), lambda i: (0, 0))],
            out_specs=[pl.BlockSpec((1, ex), lambda i: (0, 0))]
            + [pl.BlockSpec(pushed.shape, lambda i: (0, 0, 0))] * rows,
            scratch_shapes=[
                pltpu.VMEM((CHUNK * width, factors), BF16),
                pltpu.VMEM((factors + 16, CHUNK * width), F32),
                pltpu.VMEM((factors + 16, ex), BF16),
                pltpu.VMEM((ex, factors), F32),
                pltpu.VMEM((listed, factors), F32),
                pltpu.VMEM((width, factors), F32),
            ],
            name="backward",
        )(meta, values, *pieces, mine, other, labels)
        logit_list.append(logit)
        incoming = [outgoing[0]] + [across(outgoing[m], m) for m in range(1, rows)]
        parcel_shape = (ring, blocks_dev + 1, piece_rows, factors)
        keep, send = pl.pallas_call(
            functools.partial(collect_kernel, step, rows, ring, blocks_dev, listed),
            out_shape=[
                jax.ShapeDtypeStruct(parcel_shape, F32),
                jax.ShapeDtypeStruct(parcel_shape, BF16),
            ],
            in_specs=[SMEM] * (1 + rows) + [VMEM] * rows,
            out_specs=[VMEM] * 2,
            scratch_shapes=[
                pltpu.VMEM((2 * ring, blocks_dev, piece_rows, factors), F32),
                pltpu.VMEM((2 * ring * blocks_dev, factors), F32),
                pltpu.VMEM((rows * listed, factors), F32),
            ],
            name="collect",
        )(meta, *ids, *incoming)
        got = core(send)
        total = keep[0] + got[0].astype(F32)
        for s in range(1, ring):
            total = total + around((keep[s] + got[s].astype(F32)).astype(BF16), s).astype(F32)
        grad = total[:blocks_dev]
        grad_lin = total[blocks_dev]
        quarter_acc = quarter_acc + grad * grad
        quarter = quarter - learn_rate * grad / jnp.sqrt(quarter_acc)
        lin_acc = lin_acc + grad_lin * grad_lin
        lin = lin - learn_rate * grad_lin / jnp.sqrt(lin_acc)

    delta = (base - quarter).astype(BF16)
    deltas = [delta] + [across(delta, m) for m in range(1, rows)]
    some = 8
    new_table = pl.pallas_call(
        functools.partial(finish_kernel, rows),
        out_shape=jax.ShapeDtypeStruct(table.shape, F32),
        grid=(blocks_dev // some,),
        in_specs=[SMEM, pl.BlockSpec((some, width, factors), lambda i: (i, 0, 0))]
        + [pl.BlockSpec((some, piece_rows, factors), lambda i: (i, 0, 0))] * rows,
        out_specs=pl.BlockSpec((some, width, factors), lambda i: (i, 0, 0)),
        name="finish",
    )(meta, table, *deltas)
    return (new_table, lin, jnp.concatenate(logit_list, axis=0))


def solution(mesh):
    in_specs = (
        P(None, "rows", "cols"),
        P(None, "rows", "cols", None),
        P(None, "rows"),
        P("cols", None, None),
        P("cols", None, None),
        P("cols", None),
        P("cols", None),
    )
    out_specs = (P("cols", None, None), P("cols", None), P(None, "rows"))
    body = functools.partial(local, mesh.shape["rows"], mesh.shape["cols"])
    return jax.shard_map(
        body, mesh=mesh, in_specs=in_specs, out_specs=out_specs, check_vma=False
    )
```

```python
import functools

import jax
import jax.numpy as jnp
from jax import lax
from jax.experimental import pallas as pl
from jax.experimental.pallas import tpu as pltpu
from jax.sharding import PartitionSpec as P

learn_rate = 0.2
F32 = jnp.float32
BF16 = jnp.bfloat16
CHUNK = 8


VMEM = pl.BlockSpec(memory_space=pltpu.VMEM)
SMEM = pl.BlockSpec(memory_space=pltpu.SMEM)
ANY = pl.BlockSpec(memory_space=pl.ANY)


def part_of(meta, peer):
    return 2 * jnp.bitwise_xor(meta[0], peer // 2) + jnp.bitwise_xor(meta[2], peer % 2)


def split_kernel(part, meta, table, table_acc, lin, lin_acc, own_w, own_a, send_w, send_a, flip, sems):
    blocks = lin.shape[0]
    copies = []
    for n, (source, out, peer) in enumerate(
        ((table, own_w, 0), (table, send_w, 1), (table_acc, own_a, 0), (table_acc, send_a, 1))
    ):
        at = pl.multiple_of(part_of(meta, peer) * part, part)
        copies.append(
            pltpu.make_async_copy(
                source.at[:, pl.ds(at, part), :], out.at[pl.ds(0, blocks)], sems.at[n]
            )
        )
    for copy in copies:
        copy.start()
    width = lin.shape[1]
    for source, own, send, fill in ((lin, own_w, send_w, 0.0), (lin_acc, own_a, send_a, 1.0)):
        full = jnp.concatenate(
            [source[...], jnp.full((width - blocks, width), fill, F32)], axis=0
        )
        flip[...] = full.T
        for out, peer in ((own, 0), (send, 1)):
            at = pl.multiple_of(part_of(meta, peer) * part, part)
            out[blocks] = flip[pl.ds(at, part), :]
    for copy in copies:
        copy.wait()


def select_kernel(step, peers, ring, listed, *refs):
    table, codes = refs[0], refs[1]
    held = refs[2 : 2 + ring]
    outs = refs[2 + ring : 2 + ring + peers]
    pool, sems = refs[2 + ring + peers :]
    parcel, part, lanes = held[0].shape
    copies = [
        pltpu.make_async_copy(src, pool.at[pl.ds(i * parcel, parcel)], sems.at[i])
        for i, src in enumerate(held)
    ]
    for copy in copies:
        copy.start()
    pool[ring * parcel] = jnp.zeros((part, lanes), BF16)
    place = lax.broadcasted_iota(jnp.int32, (ring * lanes, peers * listed), 0)
    hot = jnp.where(place == codes[step : step + 1, :], 1.0, 0.0).astype(BF16)
    for copy in copies:
        copy.wait()
    lin = jnp.concatenate([pool[i * parcel + parcel - 1] for i in range(ring)], axis=1)
    picked = jnp.dot(lin, hot, preferred_element_type=F32).astype(BF16)
    for g in range(peers):
        outs[g][listed, :, 0:listed] = picked[:, g * listed : (g + 1) * listed]
        outs[g][listed, :, listed:] = jnp.zeros((part, lanes - listed), BF16)

        def body(k, carry, g=g):
            outs[g][k] = pool[table[step * peers + g, k]]
            return carry

        lax.fori_loop(0, listed, body, 0, unroll=16)


def gather_tiles(meta, pieces, tiles, width):
    for g, piece in enumerate(pieces):
        part = piece.shape[1]
        start = part_of(meta, g) * part
        for i in range(CHUNK):
            at = pl.multiple_of(i * width + start, part)
            tiles[pl.ds(at, part), 0:width] = piece[i]


def gather_lin(meta, lins, lin):
    for g, piece in enumerate(lins):
        part = piece.shape[1]
        at = pl.multiple_of(part_of(meta, g) * part, part)
        lin[pl.ds(at, part), :] = piece[0].astype(F32)


def forward_kernel(peers, ex, width, *refs):
    meta, values = refs[0], refs[1]
    pieces = refs[2 : 2 + peers]
    lins = refs[2 + peers : 2 + 2 * peers]
    keep, send, tiles, xv, extra, sq, lin = refs[2 + 2 * peers :]
    here = pl.program_id(0)
    gather_tiles(meta, pieces, tiles, width)

    @pl.when(here == 0)
    def _():
        xv[...] = jnp.zeros_like(xv)
        extra[...] = jnp.zeros_like(extra)
        gather_lin(meta, lins, lin)

    lane = lax.broadcasted_iota(jnp.int32, (width, width), 1)
    for i in range(CHUNK):
        cut = slice(i * width, (i + 1) * width)
        tile = tiles[cut, 0:width].astype(F32)
        flipped = (tile * tile).T
        sq[i : i + 1, :] = -0.5 * jnp.sum(flipped, axis=0, keepdims=True)
        tiles[cut, width:] = jnp.where(lane == here * CHUNK + i, lin[...], 0.0).astype(BF16)
    xv[...] += jnp.dot(values[0], tiles[...], preferred_element_type=F32)
    group = 64

    def body(g, carry):
        at = pl.multiple_of(g * group, group)
        total = extra[pl.ds(at, group), :]
        for i in range(CHUNK):
            v = values[0, pl.ds(at, group), i * width : (i + 1) * width].astype(F32)
            total = total + v * v * sq[i : i + 1, :]
        extra[pl.ds(at, group), :] = total
        return carry

    lax.fori_loop(0, ex // group, body, 0)

    @pl.when(here == pl.num_programs(0) - 1)
    def _():
        half = ex // 2
        for out, mine in ((keep, meta[2]), (send, 1 - meta[2])):
            at = pl.multiple_of(mine * half, half)
            out[:half] = xv[pl.ds(at, half), 0:width]
            tail = []
            for i in range(half // width):
                rows = pl.ds(pl.multiple_of(at + i * width, width), width)
                summed = extra[rows, :] + xv[rows, width:]
                tail.append(jnp.sum(summed.T, axis=0, keepdims=True))
            fill = out.shape[0] - half - len(tail)
            out[half:] = jnp.concatenate(tail + [jnp.zeros((fill, width), F32)], axis=0)


def backward_kernel(step, peers, ex, width, listed, *refs):
    meta, values = refs[0], refs[1]
    pieces = refs[2 : 2 + peers]
    mine, other, labels = refs[2 + peers : 5 + peers]
    logits = refs[5 + peers]
    outs = refs[6 + peers : 6 + 2 * peers]
    tiles, xvt, lhs, slope_col, lin_rows, grads = refs[6 + 2 * peers :]
    here = pl.program_id(0)
    half = ex // 2
    gather_tiles(meta, pieces, tiles, width)

    @pl.when(here == 0)
    def _():
        lin_rows[...] = jnp.zeros_like(lin_rows)
        for src, owner in ((mine, meta[2]), (other, 1 - meta[2])):
            for i in range(half // width):
                at = pl.multiple_of(owner * half + i * width, width)
                flipped = src[i * width : (i + 1) * width, :].T
                logit = src[half + i : half + i + 1, :] + 0.5 * jnp.sum(
                    flipped * flipped, axis=0, keepdims=True
                )
                label = labels[step : step + 1, pl.ds(at, width)].astype(F32)
                slope = jax.nn.sigmoid(logit) - label
                logits[:, pl.ds(at, width)] = logit
                lhs[0:width, pl.ds(at, width)] = (slope * flipped).astype(BF16)
                high = slope.astype(BF16).astype(F32)
                middle = (slope - high).astype(BF16).astype(F32)
                low = slope - high - middle
                fill = jnp.zeros((lhs.shape[0] - width - 3, width), F32)
                lhs[width:, pl.ds(at, width)] = jnp.concatenate(
                    [high, middle, low, fill], axis=0
                ).astype(BF16)
                slope_col[pl.ds(at, width), :] = jnp.broadcast_to(slope, (width, width)).T

    xvt[...] = jnp.dot(lhs[...], values[0], preferred_element_type=F32)
    group = 64

    def body(g, totals):
        at = pl.multiple_of(g * group, group)
        slope = slope_col[pl.ds(at, group), :]
        result = []
        for i in range(CHUNK):
            v = values[0, pl.ds(at, group), i * width : (i + 1) * width].astype(F32)
            term = (v * v * slope).reshape(group // 8, 8, width)
            result.append(totals[i] + jnp.sum(term, axis=0))
        return tuple(result)

    totals = lax.fori_loop(
        0, ex // group, body, tuple(jnp.zeros((8, width), F32) for _ in range(CHUNK))
    )
    weight_sq = jnp.concatenate(
        [jnp.sum(total, axis=0, keepdims=True) for total in totals], axis=0
    ).T
    row_list = []
    for i in range(CHUNK):
        cut = slice(i * width, (i + 1) * width)
        tile = tiles[cut, :].astype(F32)
        grads[...] = xvt[0:width, cut].T - tile * weight_sq[:, i : i + 1]
        for g in range(peers):
            part = pieces[g].shape[1]
            at = pl.multiple_of(part_of(meta, g) * part, part)
            outs[g][here * CHUNK + i] = grads[pl.ds(at, part), :].astype(BF16)
        row_list.append(
            xvt[width : width + 1, cut] + xvt[width + 1 : width + 2, cut] + xvt[width + 2 : width + 3, cut]
        )
    at = pl.multiple_of(here * CHUNK, CHUNK)
    lin_rows[pl.ds(at, CHUNK), :] = jnp.concatenate(row_list, axis=0)

    @pl.when(here == pl.num_programs(0) - 1)
    def _():
        grads[...] = lin_rows[...].T
        for g in range(peers):
            part = pieces[g].shape[1]
            at = pl.multiple_of(part_of(meta, g) * part, part)
            outs[g][listed] = grads[pl.ds(at, part), :].astype(BF16)


def collect_kernel(step, peers, ring, listed, *refs):
    table, codes = refs[0], refs[1]
    held = refs[2 : 2 + peers]
    keep = refs[2 + peers]
    sends = refs[3 + peers : 2 + peers + ring]
    pool, sems = refs[2 + peers + ring :]
    parcel, part, lanes = keep.shape
    blocks = parcel - 1
    copies = [
        pltpu.make_async_copy(src, pool.at[i, pl.ds(0, listed + 1)], sems.at[i])
        for i, src in enumerate(held)
    ]
    for copy in copies:
        copy.start()
    for g in range(peers):
        pool[g, listed + 1] = jnp.zeros((part, lanes), BF16)
    place = lax.broadcasted_iota(jnp.int32, (ring * lanes, peers * listed), 0)
    hot = jnp.where(place == codes[step : step + 1, :], 1.0, 0.0).astype(BF16)
    for copy in copies:
        copy.wait()
    lin = jnp.concatenate([pool[g, listed, :, 0:listed] for g in range(peers)], axis=1)
    summed = lax.dot_general(lin, hot, (((1,), (1,)), ((), ())), preferred_element_type=F32)
    for s in range(ring):
        out = keep if s == 0 else sends[s - 1]

        def body(i, carry, s=s, out=out):
            terms = [
                pool[g, table[step * peers + g, s * blocks + i]].astype(F32)
                for g in range(peers)
            ]
            while len(terms) > 1:
                terms = [a + b for a, b in zip(terms[::2], terms[1::2], strict=True)]
            out[i] = terms[0].astype(out.dtype)
            return carry

        lax.fori_loop(0, blocks, body, 0, unroll=4)
        out[blocks] = summed[:, s * lanes : (s + 1) * lanes].astype(out.dtype)


def finish_kernel(peers, *refs):
    meta, table, lin = refs[0:3]
    deltas = refs[3 : 3 + peers]
    lins = refs[3 + peers : 3 + 2 * peers]
    out, lin_out, flip = refs[3 + 2 * peers :]
    for g in range(peers):
        part = deltas[g].shape[1]
        rows = pl.ds(pl.multiple_of(part_of(meta, g) * part, part), part)
        out[:, rows, :] = table[:, rows, :] - deltas[g][...].astype(F32)

    @pl.when(pl.program_id(0) == 0)
    def _():
        gather_lin(meta, lins, flip)
        blocks = lin.shape[0]
        lin_out[...] = lin[...] - flip[...].T[0:blocks]


def local(rows, cols, values, block_ids, labels, table, table_acc, lin, lin_acc):
    steps, ex, depth = values.shape
    listed = block_ids.shape[3]
    blocks_dev, width, factors = table.shape
    ring = cols // 2
    peers = 2 * rows
    part = width // peers
    blocks = 2 * blocks_dev
    assert factors == width and blocks <= width and listed <= width and listed % CHUNK == 0

    row = lax.axis_index("rows")
    col = lax.axis_index("cols")
    home, core = col // 2, col % 2
    meta = jnp.stack([row, home, core]).astype(jnp.int32)

    def across(x, g):
        pairs = [
            (r * cols + c, (r ^ (g // 2)) * cols + (c ^ (g % 2)))
            for r in range(rows)
            for c in range(cols)
        ]
        return lax.ppermute(x, ("rows", "cols"), pairs)

    def around(x, s):
        return lax.ppermute(
            x, "cols", [(c, (c // 2 + s) % ring * 2 + c % 2) for c in range(cols)]
        )

    def beside(x, bit):
        return lax.ppermute(x, "cols", [(c, (c // 2 ^ bit) * 2 + c % 2) for c in range(cols)])

    parcel = (blocks + 1, part, factors)
    halfway = jax.ShapeDtypeStruct((blocks_dev + 1, part, factors), F32)
    own_w, own_a, send_w, send_a = pl.pallas_call(
        functools.partial(split_kernel, part),
        out_shape=[halfway] * 4,
        in_specs=[SMEM, ANY, ANY, VMEM, VMEM],
        out_specs=[VMEM] * 4,
        scratch_shapes=[pltpu.VMEM((width, width), F32), pltpu.SemaphoreType.DMA((4,))],
        name="split",
    )(meta, table, table_acc, lin, lin_acc)

    def joined(own, got):
        tail = jnp.concatenate(
            [own[blocks_dev, :, :blocks_dev], got[blocks_dev, :, :blocks_dev], own[blocks_dev, :, blocks:]],
            axis=1,
        )
        return jnp.concatenate([own[:blocks_dev], got[:blocks_dev], tail[None]], axis=0)

    weights = joined(own_w, across(send_w, 1))
    accum = joined(own_a, across(send_a, 1))
    start = weights

    mine = block_ids.reshape(1, steps, listed)
    pair = jnp.concatenate([mine, across(mine, 1)], axis=0)
    ids = jnp.concatenate([pair] + [across(pair, 2 * m) for m in range(1, rows)], axis=0)
    ids = ids.transpose(1, 0, 2)
    live = ids >= 0
    owner = ids // blocks_dev
    inner = ids % blocks_dev + jnp.where(owner % 2 == core, 0, blocks_dev)
    from_home = (home - owner // 2) % ring
    to_home = (owner // 2 - home) % ring
    pick = jnp.where(live, from_home * parcel[0] + inner, ring * parcel[0])
    pick_table = pick.reshape(steps * peers, listed)
    pick_codes = jnp.where(live, from_home * factors + inner, -1).reshape(steps, peers * listed)
    put_codes = jnp.where(live, to_home * factors + inner, -1).reshape(steps, peers * listed)
    put = jnp.where(live, to_home * blocks + inner, -1)
    hits = put[:, :, None, :] == jnp.arange(ring * blocks)[None, None, :, None]
    slot = jnp.arange(listed) - (listed + 1)
    put_table = (
        jnp.sum(jnp.where(hits, slot, 0), axis=-1) + (listed + 1)
    ).astype(jnp.int32).reshape(steps * peers, ring * blocks)

    half_rows = ex // 2 + -(-(ex // 2 // factors) // 8) * 8
    piece = jax.ShapeDtypeStruct((listed + 1, part, factors), BF16)
    half = jax.ShapeDtypeStruct((half_rows, factors), F32)
    chunk_spec = pl.BlockSpec((CHUNK, part, factors), lambda i: (i, 0, 0))
    last_spec = pl.BlockSpec((1, part, factors), lambda i: (listed, 0, 0))
    grid = listed // CHUNK
    logit_list = []

    for step in range(steps):
        values_spec = pl.BlockSpec((1, ex, CHUNK * width), lambda i, step=step: (step, 0, i))
        held = weights.astype(BF16)
        near = [held] + [around(held, s) for s in range(1, ring)]
        picked = pl.pallas_call(
            functools.partial(select_kernel, step, peers, ring, listed),
            out_shape=[piece] * peers,
            in_specs=[SMEM, VMEM] + [ANY] * ring,
            out_specs=[VMEM] * peers,
            scratch_shapes=[
                pltpu.VMEM((ring * parcel[0] + 1, part, factors), BF16),
                pltpu.SemaphoreType.DMA((ring,)),
            ],
            name="select",
        )(pick_table, pick_codes, *near)
        pieces = [picked[0]] + [across(picked[g], g) for g in range(1, peers)]
        keep, send = pl.pallas_call(
            functools.partial(forward_kernel, peers, ex, width),
            out_shape=[half, half],
            grid=(grid,),
            in_specs=[SMEM, values_spec] + [chunk_spec] * peers + [last_spec] * peers,
            out_specs=[pl.BlockSpec((half_rows, factors), lambda i: (0, 0))] * 2,
            scratch_shapes=[
                pltpu.VMEM((CHUNK * width, 2 * factors), BF16),
                pltpu.VMEM((ex, 2 * factors), F32),
                pltpu.VMEM((ex, factors), F32),
                pltpu.VMEM((CHUNK, width), F32),
                pltpu.VMEM((width, factors), F32),
            ],
            name="forward",
        )(meta, values, *pieces, *pieces)
        mine = keep + across(send, 1)
        bit = 1
        while bit < ring:
            mine = mine + beside(mine, bit)
            bit *= 2
        other = across(mine, 1)
        logit, *outgoing = pl.pallas_call(
            functools.partial(backward_kernel, step, peers, ex, width, listed),
            out_shape=[jax.ShapeDtypeStruct((1, ex), F32)] + [piece] * peers,
            grid=(grid,),
            in_specs=[SMEM, values_spec]
            + [chunk_spec] * peers
            + [pl.BlockSpec((half_rows, factors), lambda i: (0, 0))] * 2
            + [pl.BlockSpec((steps, ex), lambda i: (0, 0))],
            out_specs=[pl.BlockSpec((1, ex), lambda i: (0, 0))]
            + [pl.BlockSpec(piece.shape, lambda i: (0, 0, 0))] * peers,
            scratch_shapes=[
                pltpu.VMEM((CHUNK * width, factors), BF16),
                pltpu.VMEM((factors + 16, CHUNK * width), F32),
                pltpu.VMEM((factors + 16, ex), BF16),
                pltpu.VMEM((ex, factors), F32),
                pltpu.VMEM((width, factors), F32),
                pltpu.VMEM((width, factors), F32),
            ],
            name="backward",
        )(meta, values, *pieces, mine, other, labels)
        logit_list.append(logit)
        incoming = [outgoing[0]] + [across(outgoing[g], g) for g in range(1, peers)]
        grad, *sends = pl.pallas_call(
            functools.partial(collect_kernel, step, peers, ring, listed),
            out_shape=[jax.ShapeDtypeStruct(parcel, F32)]
            + [jax.ShapeDtypeStruct(parcel, BF16)] * (ring - 1),
            in_specs=[SMEM, VMEM] + [ANY] * peers,
            out_specs=[VMEM] * ring,
            scratch_shapes=[
                pltpu.VMEM((peers, listed + 2, part, factors), BF16),
                pltpu.SemaphoreType.DMA((peers,)),
            ],
            name="collect",
        )(put_table, put_codes, *incoming)
        for s in range(1, ring):
            grad = grad + around(sends[s - 1], s).astype(F32)
        accum = accum + grad * grad
        weights = weights - learn_rate * grad / jnp.sqrt(accum)

    delta = (start - weights).astype(BF16)
    parts = [
        jnp.concatenate(
            [
                delta[q * blocks_dev : (q + 1) * blocks_dev],
                jnp.pad(
                    delta[blocks, :, q * blocks_dev : (q + 1) * blocks_dev],
                    ((0, 0), (0, factors - blocks_dev)),
                )[None],
            ],
            axis=0,
        )
        for q in range(2)
    ]
    deltas = [parts[0]] + [across(parts[g % 2], g) for g in range(1, peers)]
    some = 8
    rest = pl.BlockSpec((1, part, factors), lambda i: (blocks_dev, 0, 0))
    whole = pl.BlockSpec(lin.shape, lambda i: (0, 0))
    new_table, new_lin = pl.pallas_call(
        functools.partial(finish_kernel, peers),
        out_shape=[jax.ShapeDtypeStruct(table.shape, F32), jax.ShapeDtypeStruct(lin.shape, F32)],
        grid=(blocks_dev // some,),
        in_specs=[SMEM, pl.BlockSpec((some, width, factors), lambda i: (i, 0, 0)), whole]
        + [pl.BlockSpec((some, part, factors), lambda i: (i, 0, 0))] * peers
        + [rest] * peers,
        out_specs=[pl.BlockSpec((some, width, factors), lambda i: (i, 0, 0)), whole],
        scratch_shapes=[pltpu.VMEM((width, factors), F32)],
        name="finish",
    )(meta, table, lin, *deltas, *deltas)
    return (new_table, new_lin, jnp.concatenate(logit_list, axis=0))


def solution(mesh):
    in_specs = (
        P(None, "rows", "cols"),
        P(None, "rows", "cols", None),
        P(None, "rows"),
        P("cols", None, None),
        P("cols", None, None),
        P("cols", None),
        P("cols", None),
    )
    out_specs = (P("cols", None, None), P("cols", None), P(None, "rows"))
    body = functools.partial(local, mesh.shape["rows"], mesh.shape["cols"])
    return jax.shard_map(
        body, mesh=mesh, in_specs=in_specs, out_specs=out_specs, check_vma=False
    )
```

```python
import functools

import jax
import jax.numpy as jnp
from jax import lax
from jax.experimental import pallas as pl
from jax.experimental.pallas import tpu as pltpu
from jax.sharding import PartitionSpec as P

learn_rate = 0.2
F32 = jnp.float32
BF16 = jnp.bfloat16
CHUNK = 8
HALVES = 2


VMEM = pl.BlockSpec(memory_space=pltpu.VMEM)
SMEM = pl.BlockSpec(memory_space=pltpu.SMEM)
ANY = pl.BlockSpec(memory_space=pl.ANY)
HBM = pl.BlockSpec(memory_space=pltpu.HBM)


def part_of(meta, peer):
    return 2 * jnp.bitwise_xor(meta[0], peer // 2) + jnp.bitwise_xor(meta[2], peer % 2)


def starts_of(meta, peers, part):
    return [(part_of(meta, g) * HALVES + h) * part for h in range(HALVES) for g in range(peers)]


def split_kernel(part, meta, full, line, fill, *refs):
    outs, flip, sems = refs[: 2 * HALVES], refs[2 * HALVES], refs[2 * HALVES + 1]
    blocks, width = line.shape
    copies = []
    for n, start in enumerate(starts_of(meta, 2, part)):
        at = pl.multiple_of(start, part)
        copies.append(
            pltpu.make_async_copy(
                full.at[:, pl.ds(at, part), :], outs[n].at[pl.ds(0, blocks)], sems.at[n]
            )
        )
        copies[-1].start()
    padded = jnp.concatenate([line[...], jnp.full((width - blocks, width), fill[0], F32)], axis=0)
    flip[...] = padded.T
    for n, start in enumerate(starts_of(meta, 2, part)):
        outs[n][blocks] = flip[pl.ds(pl.multiple_of(start, part), part), :]
    for copy in copies:
        copy.wait()


def join_kernel(own, got, out, *held):
    blocks = own.shape[0] - 1
    out[0:blocks] = own[0:blocks]
    out[blocks : 2 * blocks] = got[0:blocks]
    lane = lax.broadcasted_iota(jnp.int32, own.shape[1:], 1)
    moved = pltpu.roll(got[blocks], blocks, 1)
    mixed = jnp.where((lane >= blocks) & (lane < 2 * blocks), moved, own[blocks])
    out[2 * blocks] = mixed
    for other in held:
        other[...] = out[...].astype(BF16)


def update_kernel(ring, weights, accum, grad, *refs):
    got = refs[: ring - 1]
    new_weights, new_accum, held = refs[ring - 1 :]
    total = grad[...]
    for other in got:
        total = total + other[...].astype(F32)
    squared = accum[...] + total * total
    new_accum[...] = squared
    fresh = weights[...] - learn_rate * total / jnp.sqrt(squared)
    new_weights[...] = fresh
    held[...] = fresh.astype(BF16)


def last_kernel(ring, start, weights, accum, grad, *refs):
    got = refs[: ring - 1]
    own, other = refs[ring - 1 :]
    total = grad[...]
    for more in got:
        total = total + more[...].astype(F32)
    squared = accum[...] + total * total
    delta = start[...] - (weights[...] - learn_rate * total / jnp.sqrt(squared))
    blocks = own.shape[0] - 1
    own[0:blocks] = delta[0:blocks].astype(BF16)
    other[0:blocks] = delta[blocks : 2 * blocks].astype(BF16)
    own[blocks] = delta[2 * blocks].astype(BF16)
    other[blocks] = pltpu.roll(delta[2 * blocks], delta.shape[2] - blocks, 1).astype(BF16)


def select_kernel(step, peers, ring, listed, *refs):
    table, codes = refs[0], refs[1]
    held = refs[2 : 2 + ring]
    outs = refs[2 + ring : 2 + ring + peers]
    pool, sems = refs[2 + ring + peers :]
    parcel, part, lanes = held[0].shape
    copies = [
        pltpu.make_async_copy(src, pool.at[pl.ds(i * parcel, parcel)], sems.at[i])
        for i, src in enumerate(held)
    ]
    for copy in copies:
        copy.start()
    pool[ring * parcel] = jnp.zeros((part, lanes), BF16)
    place = lax.broadcasted_iota(jnp.int32, (ring * lanes, peers * listed), 0)
    hot = jnp.where(place == codes[step : step + 1, :], 1.0, 0.0).astype(BF16)
    for copy in copies:
        copy.wait()
    lin = jnp.concatenate([pool[i * parcel + parcel - 1] for i in range(ring)], axis=1)
    picked = jnp.dot(lin, hot, preferred_element_type=F32).astype(BF16)
    for g in range(peers):
        outs[g][listed, :, 0:listed] = picked[:, g * listed : (g + 1) * listed]
        outs[g][listed, :, listed:] = jnp.zeros((part, lanes - listed), BF16)

        def body(k, carry, g=g):
            outs[g][k] = pool[table[step * peers + g, k]]
            return carry

        lax.fori_loop(0, listed, body, 0, unroll=16)


def start_values(step, values, held, sems):
    chunks, _, columns = held.shape

    def copy(c):
        at = pl.multiple_of(c * columns, columns)
        return pltpu.make_async_copy(
            values.at[step, :, pl.ds(at, columns)], held.at[c], sems.at[c]
        )

    for c in range(chunks):
        copy(c).start()
    return copy


def gather_tiles(starts, pieces, tiles, width, first):
    for start, piece in zip(starts, pieces, strict=True):
        part = piece.shape[1]
        for i in range(CHUNK):
            at = pl.multiple_of(i * width + start, part)
            tiles[pl.ds(at, part), :] = piece[first + i].astype(F32)


def gather_lin(starts, pieces, lin):
    for start, piece in zip(starts, pieces, strict=True):
        part = piece.shape[1]
        lin[pl.ds(pl.multiple_of(start, part), part), :] = piece[piece.shape[0] - 1].astype(F32)


def forward_kernel(step, peers, *refs):
    meta, values = refs[0], refs[1]
    pieces = refs[2 : 2 + HALVES * peers]
    keep, send, held, exact, tiles, xv, extra, sq, lin, sems = refs[2 + HALVES * peers :]
    copy = start_values(step, values, held, sems)
    chunks, ex, _ = held.shape
    width = lin.shape[0]
    starts = starts_of(meta, peers, pieces[0].shape[1])
    xv[...] = jnp.zeros_like(xv)
    extra[...] = jnp.zeros_like(extra)
    gather_lin(starts, pieces, lin)
    lane = lax.broadcasted_iota(jnp.int32, (width, width), 1)
    group = 64

    def chunk(c, carry):
        gather_tiles(starts, pieces, exact, width, c * CHUNK)
        for i in range(CHUNK):
            cut = slice(i * width, (i + 1) * width)
            tile = exact[cut]
            tiles[cut, 0:width] = tile.astype(BF16)
            flipped = (tile * tile).T
            sq[i : i + 1, :] = -0.5 * jnp.sum(flipped, axis=0, keepdims=True)
            tiles[cut, width:] = jnp.where(lane == c * CHUNK + i, lin[...], 0.0).astype(BF16)
        copy(c).wait()
        xv[...] += jnp.dot(held[c], tiles[...], preferred_element_type=F32)

        for at in range(0, ex, group):
            total = extra[at : at + group, :]
            for i in range(CHUNK):
                v = held[c, at : at + group, i * width : (i + 1) * width].astype(F32)
                total = total + v * v * sq[i : i + 1, :]
            extra[at : at + group, :] = total
        return carry

    lax.fori_loop(0, chunks, chunk, 0)
    half = ex // 2
    for out, mine in ((keep, meta[2]), (send, 1 - meta[2])):
        at = pl.multiple_of(mine * half, half)
        out[:half] = xv[pl.ds(at, half), 0:width]
        tail = []
        for i in range(half // width):
            rows = pl.ds(pl.multiple_of(at + i * width, width), width)
            summed = extra[rows, :] + xv[rows, width:]
            tail.append(jnp.sum(summed.T, axis=0, keepdims=True))
        fill = out.shape[0] - half - len(tail)
        out[half:] = jnp.concatenate(tail + [jnp.zeros((fill, width), F32)], axis=0)


def backward_kernel(step, peers, listed, *refs):
    meta, values = refs[0], refs[1]
    many = HALVES * peers
    pieces = refs[2 : 2 + many]
    mine, other, labels = refs[2 + many : 5 + many]
    logits = refs[5 + many]
    outs = refs[6 + many : 6 + 2 * many]
    held, tiles, xvt, lhs, slope_col, lin_rows, grads, sems = refs[6 + 2 * many :]
    copy = start_values(step, values, held, sems)
    chunks, ex, _ = held.shape
    half = ex // 2
    width = lin_rows.shape[0]
    part = pieces[0].shape[1]
    starts = starts_of(meta, peers, part)
    lin_rows[...] = jnp.zeros_like(lin_rows)
    for src, owner in ((mine, meta[2]), (other, 1 - meta[2])):
        for i in range(half // width):
            at = pl.multiple_of(owner * half + i * width, width)
            flipped = src[i * width : (i + 1) * width, :].T
            logit = src[half + i : half + i + 1, :] + 0.5 * jnp.sum(
                flipped * flipped, axis=0, keepdims=True
            )
            label = labels[step : step + 1, pl.ds(at, width)].astype(F32)
            slope = jax.nn.sigmoid(logit) - label
            logits[:, pl.ds(at, width)] = logit
            lhs[0:width, pl.ds(at, width)] = (slope * flipped).astype(BF16)
            high = slope.astype(BF16).astype(F32)
            middle = (slope - high).astype(BF16).astype(F32)
            low = slope - high - middle
            fill = jnp.zeros((lhs.shape[0] - width - 3, width), F32)
            lhs[width:, pl.ds(at, width)] = jnp.concatenate(
                [high, middle, low, fill], axis=0
            ).astype(BF16)
            slope_col[pl.ds(at, width), :] = jnp.broadcast_to(slope, (width, width)).T
    group = 64

    def chunk(c, carry):
        gather_tiles(starts, pieces, tiles, width, c * CHUNK)
        copy(c).wait()
        xvt[...] = jnp.dot(lhs[...], held[c], preferred_element_type=F32)

        totals = [jnp.zeros((8, width), F32)] * CHUNK
        for at in range(0, ex, group):
            slope = slope_col[at : at + group, :]
            for i in range(CHUNK):
                v = held[c, at : at + group, i * width : (i + 1) * width].astype(F32)
                term = (v * v * slope).reshape(group // 8, 8, width)
                totals[i] = totals[i] + jnp.sum(term, axis=0)
        weight_sq = jnp.concatenate(
            [jnp.sum(total, axis=0, keepdims=True) for total in totals], axis=0
        ).T
        row_list = []
        for i in range(CHUNK):
            cut = slice(i * width, (i + 1) * width)
            grads[i] = xvt[0:width, cut].T - tiles[cut] * weight_sq[:, i : i + 1]
            for start, out in zip(starts, outs, strict=True):
                rows = pl.ds(pl.multiple_of(start, part), part)
                out[c * CHUNK + i] = grads[i, rows, :].astype(BF16)
            row_list.append(
                xvt[width : width + 1, cut]
                + xvt[width + 1 : width + 2, cut]
                + xvt[width + 2 : width + 3, cut]
            )
        lin_rows[pl.ds(pl.multiple_of(c * CHUNK, CHUNK), CHUNK), :] = jnp.concatenate(
            row_list, axis=0
        )
        return carry

    lax.fori_loop(0, chunks, chunk, 0)
    grads[0] = lin_rows[...].T
    for start, out in zip(starts, outs, strict=True):
        out[listed] = grads[0, pl.ds(pl.multiple_of(start, part), part), :].astype(BF16)


def collect_kernel(step, peers, ring, listed, *refs):
    table, codes = refs[0], refs[1]
    held = refs[2 : 2 + peers]
    keep = refs[2 + peers]
    sends = refs[3 + peers : 2 + peers + ring]
    pool, sems = refs[2 + peers + ring :]
    parcel, part, lanes = keep.shape
    blocks = parcel - 1
    copies = [
        pltpu.make_async_copy(src, pool.at[i, pl.ds(0, listed + 1)], sems.at[i])
        for i, src in enumerate(held)
    ]
    for copy in copies:
        copy.start()
    for g in range(peers):
        pool[g, listed + 1] = jnp.zeros((part, lanes), BF16)
    place = lax.broadcasted_iota(jnp.int32, (ring * lanes, peers * listed), 0)
    hot = jnp.where(place == codes[step : step + 1, :], 1.0, 0.0).astype(BF16)
    for copy in copies:
        copy.wait()
    lin = jnp.concatenate([pool[g, listed, :, 0:listed] for g in range(peers)], axis=1)
    summed = lax.dot_general(lin, hot, (((1,), (1,)), ((), ())), preferred_element_type=F32)
    for s in range(ring):
        out = keep if s == 0 else sends[s - 1]

        def body(i, carry, s=s, out=out):
            terms = [
                pool[g, table[step * peers + g, s * blocks + i]].astype(F32)
                for g in range(peers)
            ]
            while len(terms) > 1:
                terms = [a + b for a, b in zip(terms[::2], terms[1::2], strict=True)]
            out[i] = terms[0].astype(out.dtype)
            return carry

        lax.fori_loop(0, blocks, body, 0, unroll=8)
        out[blocks] = summed[:, s * lanes : (s + 1) * lanes].astype(out.dtype)


def finish_kernel(peers, *refs):
    meta, table, lin = refs[0:3]
    deltas = refs[3 : 3 + HALVES * peers]
    out, lin_out, flip = refs[3 + HALVES * peers :]
    blocks = lin.shape[0]
    part = deltas[0].shape[1]
    starts = starts_of(meta, peers, part)
    for start, delta in zip(starts, deltas, strict=True):
        rows = pl.ds(pl.multiple_of(start, part), part)
        out[:, rows, :] = table[:, rows, :] - delta[0:blocks].astype(F32)
    gather_lin(starts, deltas, flip)
    lin_out[...] = lin[...] - flip[...].T[0:blocks]


def local(rows, cols, values, block_ids, labels, table, table_acc, lin, lin_acc):
    steps, ex, depth = values.shape
    values = pltpu.with_memory_space_constraint(values, pltpu.HBM)
    listed = block_ids.shape[3]
    blocks_dev, width, factors = table.shape
    ring = cols // 2
    peers = 2 * rows
    part = width // (peers * HALVES)
    blocks = 2 * blocks_dev
    assert factors == width and blocks <= width and listed <= width and listed % CHUNK == 0

    row = lax.axis_index("rows")
    col = lax.axis_index("cols")
    home, core = col // 2, col % 2
    meta = jnp.stack([row, home, core]).astype(jnp.int32)

    def across(x, g):
        pairs = [
            (r * cols + c, (r ^ (g // 2)) * cols + (c ^ (g % 2)))
            for r in range(rows)
            for c in range(cols)
        ]
        return lax.ppermute(x, ("rows", "cols"), pairs)

    def around(x, s):
        return lax.ppermute(
            x, "cols", [(c, (c // 2 + s) % ring * 2 + c % 2) for c in range(cols)]
        )

    def beside(x, bit):
        return lax.ppermute(x, "cols", [(c, (c // 2 ^ bit) * 2 + c % 2) for c in range(cols)])

    def limit(mib):
        return pltpu.CompilerParams(vmem_limit_bytes=mib << 20)

    parcel = (blocks + 1, part, factors)
    wide = jax.ShapeDtypeStruct(parcel, F32)
    thin = jax.ShapeDtypeStruct(parcel, BF16)

    def split(full, line, fill):
        return pl.pallas_call(
            functools.partial(split_kernel, part),
            out_shape=[jax.ShapeDtypeStruct((blocks_dev + 1, part, factors), F32)] * (2 * HALVES),
            in_specs=[SMEM, ANY, VMEM, SMEM],
            out_specs=[VMEM] * (2 * HALVES),
            scratch_shapes=[
                pltpu.VMEM((width, width), F32),
                pltpu.SemaphoreType.DMA((2 * HALVES,)),
            ],
            compiler_params=limit(8),
            name="split",
        )(meta, full, line, jnp.full((1,), fill, F32))

    def join(own, send, thin_too):
        shapes = [wide, thin] if thin_too else [wide]
        return pl.pallas_call(
            join_kernel,
            out_shape=shapes,
            in_specs=[VMEM] * 2,
            out_specs=[VMEM] * len(shapes),
            compiler_params=limit(8),
            name="join",
        )(own, across(send, 1))

    both = split(table, lin, 0.0)
    first = [join(both[2 * h], both[2 * h + 1], True) for h in range(HALVES)]
    weights = [pair[0] for pair in first]
    held = [pair[1] for pair in first]
    start = weights
    table_acc, lin_acc, block_ids, held = lax.optimization_barrier(
        (table_acc, lin_acc, block_ids, held)
    )
    both = split(table_acc, lin_acc, 1.0)
    accum = [join(both[2 * h], both[2 * h + 1], False)[0] for h in range(HALVES)]

    mine = block_ids.reshape(1, steps, listed)
    pair = jnp.concatenate([mine, across(mine, 1)], axis=0)
    ids = jnp.concatenate([pair] + [across(pair, 2 * m) for m in range(1, rows)], axis=0)
    ids = ids.transpose(1, 0, 2)
    live = ids >= 0
    owner = ids // blocks_dev
    inner = ids % blocks_dev + jnp.where(owner % 2 == core, 0, blocks_dev)
    from_home = (home - owner // 2) % ring
    to_home = (owner // 2 - home) % ring
    pick = jnp.where(live, from_home * parcel[0] + inner, ring * parcel[0])
    pick_table = pick.reshape(steps * peers, listed)
    pick_codes = jnp.where(live, from_home * factors + inner, -1).reshape(steps, peers * listed)
    put_codes = jnp.where(live, to_home * factors + inner, -1).reshape(steps, peers * listed)
    put = jnp.where(live, to_home * blocks + inner, -1)
    hits = put[:, :, None, :] == jnp.arange(ring * blocks)[None, None, :, None]
    slot = jnp.arange(listed) - (listed + 1)
    put_table = (
        jnp.sum(jnp.where(hits, slot, 0), axis=-1) + (listed + 1)
    ).astype(jnp.int32).reshape(steps * peers, ring * blocks)

    half_rows = ex // 2 + -(-(ex // 2 // factors) // 8) * 8
    piece = jax.ShapeDtypeStruct((listed + 1, part, factors), BF16)
    half = jax.ShapeDtypeStruct((half_rows, factors), F32)
    chunks = listed // CHUNK
    stream = [pltpu.VMEM((chunks, ex, CHUNK * width), BF16)]
    stream_sems = [pltpu.SemaphoreType.DMA((chunks,))]
    many = HALVES * peers
    logit_list = []

    for step in range(steps):
        pieces = []
        near = [[held[h]] + [around(held[h], s) for s in range(1, ring)] for h in range(HALVES)]
        for h in range(HALVES):
            picked = pl.pallas_call(
                functools.partial(select_kernel, step, peers, ring, listed),
                out_shape=[piece] * peers,
                in_specs=[SMEM, VMEM] + [ANY] * ring,
                out_specs=[VMEM] * peers,
                scratch_shapes=[
                    pltpu.VMEM((ring * parcel[0] + 1, part, factors), BF16),
                    pltpu.SemaphoreType.DMA((ring,)),
                ],
                compiler_params=limit(32),
                name="select",
            )(pick_table, pick_codes, *near[h])
            pieces += [picked[0]] + [across(picked[g], g) for g in range(1, peers)]
        keep, send = pl.pallas_call(
            functools.partial(forward_kernel, step, peers),
            out_shape=[half, half],
            in_specs=[SMEM, HBM] + [VMEM] * many,
            out_specs=[VMEM] * 2,
            scratch_shapes=stream
            + [
                pltpu.VMEM((CHUNK * width, factors), F32),
                pltpu.VMEM((CHUNK * width, 2 * factors), BF16),
                pltpu.VMEM((ex, 2 * factors), F32),
                pltpu.VMEM((ex, factors), F32),
                pltpu.VMEM((CHUNK, width), F32),
                pltpu.VMEM((width, factors), F32),
            ]
            + stream_sems,
            compiler_params=limit(32),
            name="forward",
        )(meta, values, *pieces)
        mine = keep + across(send, 1)
        bit = 1
        while bit < ring:
            mine = mine + beside(mine, bit)
            bit *= 2
        other = across(mine, 1)
        logit, *outgoing = pl.pallas_call(
            functools.partial(backward_kernel, step, peers, listed),
            out_shape=[jax.ShapeDtypeStruct((1, ex), F32)] + [piece] * many,
            in_specs=[SMEM, HBM] + [VMEM] * (many + 3),
            out_specs=[VMEM] * (1 + many),
            scratch_shapes=stream
            + [
                pltpu.VMEM((CHUNK * width, factors), F32),
                pltpu.VMEM((factors + 16, CHUNK * width), F32),
                pltpu.VMEM((factors + 16, ex), BF16),
                pltpu.VMEM((ex, factors), F32),
                pltpu.VMEM((width, factors), F32),
                pltpu.VMEM((CHUNK, width, factors), F32),
            ]
            + stream_sems,
            compiler_params=limit(32),
            name="backward",
        )(meta, values, *pieces, mine, other, labels)
        logit_list.append(logit)
        incoming = [
            outgoing[h * peers + g] if g == 0 else across(outgoing[h * peers + g], g)
            for h in range(HALVES)
            for g in range(peers)
        ]
        sums = []
        for h in range(HALVES):
            keep_h, *sends = pl.pallas_call(
                functools.partial(collect_kernel, step, peers, ring, listed),
                out_shape=[wide] + [thin] * (ring - 1),
                in_specs=[SMEM, VMEM] + [ANY] * peers,
                out_specs=[VMEM] * ring,
                scratch_shapes=[
                    pltpu.VMEM((peers, listed + 2, part, factors), BF16),
                    pltpu.SemaphoreType.DMA((peers,)),
                ],
                compiler_params=limit(32),
                name="collect",
            )(put_table, put_codes, *incoming[h * peers : (h + 1) * peers])
            sums.append([keep_h] + [around(sends[s - 1], s) for s in range(1, ring)])
        last = step == steps - 1
        if last:
            kernel, shapes, extra = last_kernel, None, start
            shapes = [jax.ShapeDtypeStruct((blocks_dev + 1, part, factors), BF16)] * 2
        else:
            kernel, shapes = update_kernel, [wide, wide, thin]
        results = []
        for h in range(HALVES):
            operands = ([start[h]] if last else []) + [weights[h], accum[h]] + sums[h]
            results.append(
                pl.pallas_call(
                    functools.partial(kernel, ring),
                    out_shape=shapes,
                    in_specs=[VMEM] * len(operands),
                    out_specs=[VMEM] * len(shapes),
                    compiler_params=limit(16),
                    name="update",
                )(*operands)
            )
        if not last:
            weights, accum, held = (list(group) for group in zip(*results, strict=True))

    deltas = [
        results[h][0] if g == 0 else across(results[h][g % 2], g)
        for h in range(HALVES)
        for g in range(peers)
    ]
    new_table, new_lin = pl.pallas_call(
        functools.partial(finish_kernel, peers),
        out_shape=[jax.ShapeDtypeStruct(table.shape, F32), jax.ShapeDtypeStruct(lin.shape, F32)],
        in_specs=[SMEM] + [VMEM] * (2 + many),
        out_specs=[VMEM] * 2,
        scratch_shapes=[pltpu.VMEM((width, factors), F32)],
        compiler_params=limit(16),
        name="finish",
    )(meta, table, lin, *deltas)
    return (new_table, new_lin, jnp.concatenate(logit_list, axis=0))


def solution(mesh):
    in_specs = (
        P(None, "rows", "cols"),
        P(None, "rows", "cols", None),
        P(None, "rows"),
        P("cols", None, None),
        P("cols", None, None),
        P("cols", None),
        P("cols", None),
    )
    out_specs = (P("cols", None, None), P("cols", None), P(None, "rows"))
    body = functools.partial(local, mesh.shape["rows"], mesh.shape["cols"])
    return jax.shard_map(
        body, mesh=mesh, in_specs=in_specs, out_specs=out_specs, check_vma=False
    )
```
